128 devices in a mesh: row: 8 (over z_hi, y), col: 16 (over z_lo, x, core).
Axes of the slice: x: 4, y: 4, z: 4 (z_hi: 2, z_lo: 2; z = z_hi * 2 + z_lo), core: 2. Of those that a mesh axis runs over, the one named last changes fastest.
Arguments:
- tokens: bfloat16 [2, 128, 16384], P(None, 'col', 'row'), may hold values from -6 to 6
- gate_weight: bfloat16 [16384, 26624], P(('row', 'col')), may hold values from -0.046875 to 0.046875
- up_weight: bfloat16 [16384, 26624], P(('row', 'col')), may hold values from -0.046875 to 0.046875
- down_weight: bfloat16 [16384, 26624], P(('row', 'col')), may hold values from -0.0390625 to 0.0390625
Outputs:
- block_out: bfloat16 [2, 128, 16384], P(None, 'col', 'row')
The draws below stay inside these ranges and needn't reach their ends.
All inputs are finite; a program needn't handle non-finite values.
Results may differ from the reference program's by a relative error of at most 0.028.
Values may be sent and summed in bfloat16 or wider, within the bound.
A program may use at most 128 MiB of HBM per device.

```python
import jax
import jax.numpy as jnp
from jax import lax

D = 16384
FF = 26624
MB = 2
TOKENS = 128
N_ROW = 8
N_COL = 16


def block_scale(rng, dims, split, least, top_value):
    gain = 1.0
    for position, blocks in split:
        steps = jax.random.uniform(jax.random.fold_in(jax.random.fold_in(rng, 6), position), (blocks,), jnp.float32, least / len(split), top_value / len(split))
        gain = gain * jnp.repeat(jnp.exp(steps), dims[position] // blocks).reshape((-1,) + (1,) * (len(dims) - 1 - position))
    return gain


def scatter_about(own_key, dims, deviation, most, split=(), dtype=jnp.bfloat16):
    result = jax.random.normal(own_key, dims, jnp.float32) * deviation
    if len(split) > 0:
        result = block_scale(own_key, dims, split, -0.22, 0.18) * result
    return jnp.clip(result, min=-most, max=most).astype(dtype)


def setup_inputs(seed: int = 0) -> dict:
    arg_keys = jax.random.split(jax.random.key(seed), 5)
    tokens = scatter_about(arg_keys[0], (MB, TOKENS, D), 1.0, 6.0, ((1, 16), (2, 8)))
    gate_weight = scatter_about(arg_keys[1], (D, FF), D ** -0.5, 0.046875, ((0, 128),))
    up_weight = scatter_about(arg_keys[2], (D, FF), D ** -0.5, 0.046875, ((0, 128),))
    down_weight = scatter_about(arg_keys[3], (D, FF), FF ** -0.5, 0.0390625, ((0, 128),))
    return {"tokens": tokens, "gate_weight": gate_weight, "up_weight": up_weight, "down_weight": down_weight}


def rounded(value):
    return lax.optimization_barrier(value.astype(jnp.bfloat16)).astype(jnp.float32)


def reference(tokens, gate_weight, up_weight, down_weight):
    row_width = D // N_ROW
    col_width = FF // N_COL
    results = []
    for batch_index in range(MB):
        batch = tokens[batch_index]
        gate = jnp.zeros((TOKENS, FF), jnp.float32)
        up_sum = jnp.zeros((TOKENS, FF), jnp.float32)
        for block in range(N_ROW):
            lower = block * row_width
            piece = batch[:, lower:lower + row_width]
            gate = gate + rounded(jnp.dot(piece, gate_weight[lower:lower + row_width], preferred_element_type=jnp.float32))
            up_sum = up_sum + rounded(jnp.dot(piece, up_weight[lower:lower + row_width], preferred_element_type=jnp.float32))
        hidden = (jax.nn.silu(gate) * up_sum).astype(jnp.bfloat16)
        summed = jnp.zeros((TOKENS, D), jnp.float32)
        for block in range(N_COL):
            lower = block * col_width
            term = lax.dot_general(hidden[:, lower:lower + col_width], down_weight[:, lower:lower + col_width], (((1,), (1,)), ((), ())), preferred_element_type=jnp.float32)
            summed = summed + rounded(term)
        results.append(summed.astype(jnp.bfloat16))
    return jnp.stack(results, 0)
```

```python
import jax
import jax.numpy as jnp
from jax import lax
from jax.experimental import pallas as pl
from jax.experimental.pallas import tpu as pltpu
from jax.sharding import PartitionSpec as P

MESH = pl.DeviceIdType.MESH
SIDE = 4
TILE = 128
WAVES = ((9, 9, 8),)
GATE_OF = (0, 1, 0, 1, 0, 1)
LAG = 3


class Region:
    def __init__(self, wave, color, tiles, offset):
        self.wave, self.color, self.width, self.offset = wave, color, tiles * TILE, offset
        self.axes = tuple((color + i) % 3 for i in range(3))


def regions_of(units):
    regions, offset = [], 0
    for wave, tiles in enumerate(WAVES):
        for color, count in enumerate(tiles):
            region = Region(wave, color, count, offset)
            regions.append(region)
            offset += SIDE * region.width
    assert offset == units
    return regions


def multiple(value, of):
    return pl.multiple_of(value, of)


def kernel(regions, half, *refs):
    tokens, gate_hbm, up_hbm, down_hbm, out = refs[:5]
    weights, gathered, parts, inbox, total = refs[5:10]
    (tok_send, tok_recv, tok_own, out_send, out_recv, w_own, w_send, w_recv, d_own, d_send, d_recv) = refs[10:21]
    (red_send, red_recv, all_send, all_recv) = refs[21:25]
    bufs = refs[25:]
    for index, region in enumerate(regions):
        region.index = index
        region.sums, region.box1, region.box2, region.box3, region.hidden = bufs[5 * index : 5 * index + 5]
        region.boxes = (region.box1, region.box2, region.box3)

    row, col = lax.axis_index("row"), lax.axis_index("col")
    core = lax.rem(col, 2)
    place = (
        lax.rem(lax.div(col, 2), 4),
        lax.rem(row, 4),
        lax.div(row, 4) * 2 + lax.div(col, 8),
    )
    cols = 16
    chip = lax.div(col, 2)

    def device(x, y, z):
        return (lax.div(z, 2) * 4 + y, lax.rem(z, 2) * 8 + x * 2 + core)

    def turned(value, step):
        return lax.rem(value + (step + SIDE), SIDE)

    def neighbour(axis, step):
        at = list(place)
        at[axis] = turned(at[axis], step)
        return device(*at)

    partner = (row, lax.rem(chip * 2 + 1 - core, 16))

    def peer(step):
        return lax.rem(col + step, cols)

    hbm = (gate_hbm, up_hbm, down_hbm)

    def weight_columns(region, quarter):
        if quarter is None:
            return region.offset, SIDE * region.width
        return region.offset + quarter * region.width, region.width

    def weight_copy(region, matrix, quarter, sems, remote):
        start, size = weight_columns(region, quarter)
        rows = pl.ds(multiple(core * TILE, TILE), TILE)
        here = weights.at[matrix, rows, pl.ds(multiple(start, TILE), size)]
        which = 1 - core if remote else core
        source = hbm[matrix].at[:, pl.ds(multiple(which * half + start, TILE), size)]
        own, send, recv = sems
        if not remote:
            return pltpu.make_async_copy(source, here, own)
        return pltpu.make_async_remote_copy(
            src_ref=source, dst_ref=here, send_sem=send, recv_sem=recv, device_id=partner, device_id_type=MESH
        )

    def quarters(region):
        at = place[region.axes[0]]
        return (turned(at, 2), turned(at, 1), turned(at, -1), at)

    def term_weight(region, matrix, position, remote):
        sem = position * 2 + matrix
        quarter = quarters(region)[position] if region.wave == 0 else None
        index = (region.index, sem)
        return weight_copy(region, matrix, quarter, (w_own.at[index], w_send.at[index], w_recv.at[index]), remote)

    def down_weight(region, remote):
        index = region.index
        return weight_copy(region, 2, None, (d_own.at[index], d_send.at[index], d_recv.at[index]), remote)

    def positions(region):
        return range(4) if region.wave == 0 else range(1)

    def weight_order():
        for position in range(4):
            for region in regions:
                if region.wave == 0:
                    yield region, position
        for region in regions:
            if region.wave > 0:
                yield region, 0

    def token_copy(step):
        to = peer(step)
        return pltpu.make_async_remote_copy(
            src_ref=tokens.at[:, pl.ds(multiple(lax.div(to, 2) * 256, 256), 256)],
            dst_ref=gathered.at[col],
            send_sem=tok_send.at[step],
            recv_sem=tok_recv.at[step],
            device_id=(row, to),
            device_id_type=MESH,
        )

    def token_arrival(step):
        slot = gathered.at[lax.rem(col + cols - step, cols)]
        return pltpu.make_async_remote_copy(
            src_ref=slot, dst_ref=slot, send_sem=tok_send.at[step], recv_sem=tok_recv.at[step],
            device_id=(row, peer(step)), device_id_type=MESH,
        )

    def out_copy(step):
        to = peer(step)
        return pltpu.make_async_remote_copy(
            src_ref=parts.at[to],
            dst_ref=inbox.at[col],
            send_sem=out_send.at[step],
            recv_sem=out_recv.at[step],
            device_id=(row, to),
            device_id_type=MESH,
        )

    def out_arrival(step):
        slot = inbox.at[lax.rem(col + cols - step, cols)]
        return pltpu.make_async_remote_copy(
            src_ref=slot, dst_ref=slot, send_sem=out_send.at[step], recv_sem=out_recv.at[step],
            device_id=(row, peer(step)), device_id_type=MESH,
        )

    def at_stage(region, stage):
        return place[region.axes[stage]]

    def sums_view(region, stage, matrix, quarter):
        if stage == 0:
            return region.sums.at[matrix, quarter]
        first = at_stage(region, 0)
        if stage == 1:
            return region.sums.at[matrix, first, pl.ds(multiple(quarter * 64, 64), 64)]
        start = at_stage(region, 1) * 64 + quarter * 16
        return region.sums.at[matrix, first, pl.ds(multiple(start, 16), 16)]

    def red_copy(region, stage, slot):
        step = 1 if slot < 3 else -1
        at = at_stage(region, stage)
        quarter = turned(at, 2) if slot % 3 == 0 else turned(at, step)
        index = (region.index, stage * 6 + slot)
        return pltpu.make_async_remote_copy(
            src_ref=sums_view(region, stage, GATE_OF[slot], quarter),
            dst_ref=region.boxes[stage].at[slot],
            send_sem=red_send.at[index],
            recv_sem=red_recv.at[index],
            device_id=neighbour(region.axes[stage], step),
            device_id_type=MESH,
        )

    def add_rows(target, *terms):
        rows = target.shape[0]

        @pl.loop(0, rows // 16)
        def _(block):
            at = pl.ds(multiple(block * 16, 16), 16)
            value = target[at, :].astype(jnp.float32)
            for term in terms:
                value = value + term[at, :].astype(jnp.float32)
            target[at, :] = value.astype(jnp.bfloat16)

    def terms(region, quarter):
        columns = pl.ds(multiple(region.offset + quarter * region.width, TILE), region.width)

        @pl.loop(0, 2)
        def _(matrix):
            block = gathered[...].reshape(256, 256)
            region.sums[matrix, quarter] = jnp.dot(
                block, weights[matrix, :, columns], preferred_element_type=jnp.float32
            ).astype(jnp.bfloat16)

    def wait_weights(region, position):
        for matrix in range(2):
            term_weight(region, matrix, position, False).wait()
            term_weight(region, matrix, position, True).wait_recv()

    def task_first(region):
        wait_weights(region, 0)
        terms(region, quarters(region)[0])
        red_copy(region, 0, 0).start()
        red_copy(region, 0, 3).start()

    def task_second(region):
        for position, slot in ((1, 1), (2, 4), (3, None)):
            if region.wave == 0:
                wait_weights(region, position)
            terms(region, quarters(region)[position])
            if slot is not None:
                red_copy(region, 0, slot).start()

    def task_relay(stage):
        def run(region):
            at = at_stage(region, stage)
            for slot, step in ((0, 1), (3, -1)):
                red_copy(region, stage, slot).wait_recv()
                add_rows(sums_view(region, stage, GATE_OF[slot], turned(at, step)), region.boxes[stage].at[slot])
                red_copy(region, stage, slot + 2).start()

        return run

    def arrived(region, stage):
        for slot in (1, 4, 2, 5):
            red_copy(region, stage, slot).wait_recv()

    def task_settle(stage):
        def run(region):
            at = at_stage(region, stage)
            arrived(region, stage)
            box = region.boxes[stage]
            add_rows(sums_view(region, stage, 0, at), box.at[2], box.at[4])
            add_rows(sums_view(region, stage, 1, at), box.at[1], box.at[5])
            for slot in (0, 3, 1, 4):
                red_copy(region, stage + 1, slot).start()

        return run

    def hidden_view(region, stage, quarter, part=None):
        if stage == 0:
            if part is None:
                return region.hidden.at[quarter]
            return region.hidden.at[quarter, pl.ds(part * 128, 128)]
        first = at_stage(region, 0)
        if stage == 1:
            start, size = quarter * 64, 64
            if part is not None:
                start, size = start + part * 32, 32
            return region.hidden.at[first, pl.ds(multiple(start, size), size)]
        start = at_stage(region, 1) * 64 + quarter * 16
        return region.hidden.at[first, pl.ds(multiple(start, 16), 16)]

    def forwards(region, stage):
        return (2, 3) if stage < 2 else (2 + (region.color + region.wave) % 2,)

    def all_copy(region, stage, slot, arrival=False):
        step = 1 if slot % 2 == 0 else -1
        at = at_stage(region, stage)
        if slot < 2:
            quarter, part = at, None
            landed = turned(at, -step)
        else:
            quarter, part = turned(at, -step), (slot - 2 if stage < 2 else None)
            landed = turned(at, 2)
        view = hidden_view(region, stage, landed if arrival else quarter, part)
        index = (region.index, stage * 4 + slot)
        return pltpu.make_async_remote_copy(
            src_ref=view, dst_ref=view, send_sem=all_send.at[index], recv_sem=all_recv.at[index],
            device_id=neighbour(region.axes[stage], step), device_id_type=MESH,
        )

    def task_hidden(region):
        arrived(region, 2)
        at = at_stage(region, 2)
        box = region.box3
        gate = sums_view(region, 2, 0, at)[...].astype(jnp.float32)
        gate = gate + box[2].astype(jnp.float32) + box[4].astype(jnp.float32)
        up = sums_view(region, 2, 1, at)[...].astype(jnp.float32)
        up = up + box[1].astype(jnp.float32) + box[5].astype(jnp.float32)
        hidden_view(region, 2, at)[...] = (gate / (1.0 + jnp.exp(-gate)) * up).astype(jnp.bfloat16)
        for slot in (0, 1):
            all_copy(region, 2, slot).start()

    def task_forward(stage):
        def run(region):
            for slot in (0, 1):
                all_copy(region, stage, slot, True).wait_recv()
            for slot in forwards(region, stage):
                all_copy(region, stage, slot).start()

        return run

    def task_gathered(stage):
        def run(region):
            for slot in forwards(region, stage):
                all_copy(region, stage, slot, True).wait_recv()
            for slot in (0, 1):
                all_copy(region, stage - 1, slot).start()

        return run

    def project(region, quarter):
        columns = pl.ds(multiple(region.offset + quarter * region.width, TILE), region.width)
        total[...] += lax.dot_general(
            region.hidden[quarter], weights[2, :, columns], (((1,), (1,)), ((), ())), preferred_element_type=jnp.float32
        )

    def task_project(region):
        down_weight(region, False).wait()
        down_weight(region, True).wait_recv()
        for slot in forwards(region, 0):
            all_copy(region, 0, slot, True).wait_recv()

        @pl.loop(0, SIDE)
        def _(quarter):
            project(region, quarter)

    tasks = (
        task_first, task_second, task_relay(0), task_settle(0), task_relay(1), task_settle(1), task_relay(2),
        task_hidden, task_forward(2), task_gathered(2), task_forward(1), task_gathered(1), task_forward(0), task_project,
    )

    for region, position in weight_order():
        for matrix in range(2):
            term_weight(region, matrix, position, False).start()
    own_tokens = pltpu.make_async_copy(
        tokens.at[:, pl.ds(multiple(chip * 256, 256), 256)], gathered.at[col], tok_own
    )
    own_tokens.start()

    barrier = pltpu.get_barrier_semaphore()
    for step in range(1, cols):
        pl.semaphore_signal(barrier, inc=1, device_id=(row, peer(step)), device_id_type=MESH)
    for axis in (1, 2):
        for step in (1, -1):
            pl.semaphore_signal(barrier, inc=1, device_id=neighbour(axis, step), device_id_type=MESH)
    pl.semaphore_wait(barrier, cols - 1 + 4)

    for step in range(1, cols):
        token_copy(step).start()
    for region, position in weight_order():
        for matrix in range(2):
            term_weight(region, matrix, position, True).start()
    for region in regions:
        down_weight(region, False).start()
        down_weight(region, True).start()

    total[...] = jnp.zeros_like(total)
    own_tokens.wait()
    for step in range(1, cols):
        token_arrival(step).wait_recv()

    waves = len(WAVES)
    for tick in range(len(tasks) + LAG * (waves - 1)):
        for wave in range(waves):
            number = tick - LAG * wave
            if 0 <= number < len(tasks):
                for region in regions:
                    if region.wave == wave:
                        tasks[number](region)

    parts[...] = total[...].astype(jnp.bfloat16).reshape(cols, 16, 256)
    for step in range(1, cols):
        out_copy(step).start()
    inbox[col] = parts[col]
    for step in range(1, cols):
        out_arrival(step).wait_recv()
    for block in range(cols // 2):
        out[:, block * 256 : (block + 1) * 256] = (
            inbox[2 * block].astype(jnp.float32) + inbox[2 * block + 1].astype(jnp.float32)
        ).astype(jnp.bfloat16)

    for step in range(1, cols):
        token_copy(step).wait_send()
        out_copy(step).wait_send()
    for region in regions:
        for position in positions(region):
            for matrix in range(2):
                term_weight(region, matrix, position, True).wait_send()
        down_weight(region, True).wait_send()
        for stage in range(3):
            for slot in range(6):
                red_copy(region, stage, slot).wait_send()
            for slot in (0, 1) + tuple(forwards(region, stage)):
                all_copy(region, stage, slot).wait_send()


def on_device(tokens, gate_weight, up_weight, down_weight):
    batches, block, width = tokens.shape
    units = gate_weight.shape[1]
    half = units // 2
    regions = regions_of(half)
    count = len(regions)
    bf16 = jnp.bfloat16
    dma = pltpu.SemaphoreType.DMA

    scratch = [
        pltpu.VMEM((3, 256, half), bf16),
        pltpu.VMEM((16, 16, 256), bf16),
        pltpu.VMEM((16, 16, 256), bf16),
        pltpu.VMEM((16, 16, 256), bf16),
        pltpu.VMEM((256, 256), jnp.float32),
        dma((16,)), dma((16,)), dma(()), dma((16,)), dma((16,)),
        dma((count, 8)), dma((count, 8)), dma((count, 8)),
        dma((count,)), dma((count,)), dma((count,)),
        dma((count, 18)), dma((count, 18)), dma((count, 12)), dma((count, 12)),
    ]
    for region in regions:
        w = region.width
        scratch += [
            pltpu.VMEM((2, 4, 256, w), bf16),
            pltpu.VMEM((6, 256, w), bf16),
            pltpu.VMEM((6, 64, w), bf16),
            pltpu.VMEM((6, 16, w), bf16),
            pltpu.VMEM((4, 256, w), bf16),
        ]

    anywhere = pl.BlockSpec(memory_space=pl.ANY)
    out = pl.pallas_call(
        lambda *refs: kernel(regions, half, *refs),
        out_shape=jax.ShapeDtypeStruct((batches * block, width), bf16),
        in_specs=[anywhere] * 4,
        out_specs=pl.BlockSpec(memory_space=pltpu.VMEM),
        scratch_shapes=scratch,
        name="ffn",
        compiler_params=pltpu.CompilerParams(
            collective_id=0, has_side_effects=True, vmem_limit_bytes=67_000_000
        ),
    )(tokens.reshape(batches * block, width), gate_weight, up_weight, down_weight)
    return out.reshape(batches, block, width)


def solution(mesh):
    spread = P(("row", "col"), None)
    return jax.shard_map(
        on_device,
        mesh=mesh,
        in_specs=(P(None, "col", "row"), spread, spread, spread),
        out_specs=P(None, "col", "row"),
        check_vma=False,
    )
```

```python
import jax
import jax.numpy as jnp
from jax import lax
from jax.experimental import pallas as pl
from jax.experimental.pallas import tpu as pltpu
from jax.sharding import PartitionSpec as P

MESH = pl.DeviceIdType.MESH
SIDE = 4
TILE = 128
WAVES = ((3, 3, 3), (3, 3, 3), (3, 3, 2))
GATE_OF = (1, 0, 0, 1, 0, 1)
STEP_OF = (1, 1, -1, -1, 1, -1)
LAG = 1
ROWS = (256, 64, 16)


class Region:
    def __init__(self, wave, color, tiles, offset):
        self.wave, self.color, self.width, self.offset = wave, color, tiles * TILE, offset
        self.axes = tuple((color + i) % 3 for i in range(3))
        self.pieces = SIDE if wave == 0 else 1


def regions_of(units):
    regions, offset = [], 0
    for wave, tiles in enumerate(WAVES):
        for color, count in enumerate(tiles):
            if count == 0:
                continue
            region = Region(wave, color, count, offset)
            regions.append(region)
            offset += SIDE * region.width
    assert offset == units
    return regions


def multiple(value, of):
    return pl.multiple_of(value, of)


def kernel(regions, half, *refs):
    tokens, gate_hbm, up_hbm, down_hbm, out = refs[:5]
    weights, gathered, parts, inbox, total = refs[5:10]
    exchange, w_own, w_send, w_recv, d_own, d_send, d_recv, red_send, red_recv, all_send, all_recv = refs[10:21]
    bufs = refs[21:]
    first = 0
    for index, region in enumerate(regions):
        region.index, region.first = index, first
        first += region.pieces
        region.sums, region.box1, region.box2, region.box3, region.hidden = bufs[5 * index : 5 * index + 5]
        region.boxes = (region.box1, region.box2, region.box3)

    row, col = lax.axis_index("row"), lax.axis_index("col")
    core = lax.rem(col, 2)
    chip = lax.div(col, 2)
    place = (lax.rem(chip, 4), lax.rem(row, 4), lax.div(row, 4) * 2 + lax.div(col, 8))
    cols = 16

    def device(x, y, z):
        return (lax.div(z, 2) * 4 + y, lax.rem(z, 2) * 8 + x * 2 + core)

    around = [[lax.rem(place[axis] + step, SIDE) for step in range(SIDE)] for axis in range(3)]
    near = {}
    for axis in range(3):
        for step in (1, -1):
            at = list(place)
            at[axis] = around[axis][step]
            near[axis, step] = device(*at)
    partner = (row, chip * 2 + 1 - core)
    peers = [lax.rem(col + step, cols) for step in range(cols)]

    def drain(ref, sem):
        pltpu.make_async_copy(ref, ref, sem).wait()

    hbm = (gate_hbm, up_hbm, down_hbm)

    def weight_columns(region, quarter):
        if quarter is None:
            return region.offset, SIDE * region.width
        return region.offset + quarter * region.width, region.width

    def weight_copy(region, matrix, quarter, sems, remote):
        start, size = weight_columns(region, quarter)
        rows = pl.ds(multiple(core * TILE, TILE), TILE)
        here = weights.at[matrix, rows, pl.ds(multiple(start, TILE), size)]
        which = 1 - core if remote else core
        source = hbm[matrix].at[:, pl.ds(multiple(which * half + start, TILE), size)]
        own, send, recv = sems
        if not remote:
            return pltpu.make_async_copy(source, here, own)
        return pltpu.make_async_remote_copy(
            src_ref=source, dst_ref=here, send_sem=send, recv_sem=recv, device_id=partner, device_id_type=MESH
        )

    def quarters(region):
        return [around[region.axes[0]][step] for step in (2, 1, -1, 0)]

    def term_weight(region, matrix, position, remote):
        quarter = quarters(region)[position] if region.wave == 0 else None
        index = region.first + position
        sems = (w_own.at[index], w_send.at[region.index], w_recv.at[index])
        return weight_copy(region, matrix, quarter, sems, remote)

    def wait_weights(region, position):
        start, size = weight_columns(region, quarters(region)[position] if region.wave == 0 else None)
        both = weights.at[pl.ds(0, 2), pl.ds(0, TILE), pl.ds(multiple(start, TILE), size)]
        drain(both, w_own.at[region.first + position])
        drain(both, w_recv.at[region.first + position])

    def down_weight(region, remote):
        index = region.index
        return weight_copy(region, 2, None, (d_own.at[index], d_send.at[index], d_recv.at[index]), remote)

    def weight_order():
        for position in range(4):
            for region in regions:
                if region.wave == 0:
                    yield region, position
        for region in regions:
            if region.wave > 0:
                yield region, 0

    def token_copy(step):
        to = peers[step]
        return pltpu.make_async_remote_copy(
            src_ref=tokens.at[:, pl.ds(multiple(lax.div(to, 2) * 256, 256), 256)],
            dst_ref=gathered.at[col],
            send_sem=exchange.at[0],
            recv_sem=exchange.at[1],
            device_id=(row, to),
            device_id_type=MESH,
        )

    def out_copy(step):
        to = peers[step]
        return pltpu.make_async_remote_copy(
            src_ref=parts.at[to],
            dst_ref=inbox.at[col],
            send_sem=exchange.at[2],
            recv_sem=exchange.at[3],
            device_id=(row, to),
            device_id_type=MESH,
        )

    others = pl.ds(0, cols - 1)

    def at_stage(region, stage, step=0):
        return around[region.axes[stage]][step]

    def rows_from(region, stage, step):
        if stage == 1:
            return multiple(at_stage(region, 1, step) * 64, 64)
        return multiple(at_stage(region, 1) * 64 + at_stage(region, 2, step) * 16, 16)

    def sums_view(region, stage, matrix, step):
        if stage == 0:
            return region.sums.at[matrix, at_stage(region, 0, step)]
        return region.sums.at[matrix, at_stage(region, 0), pl.ds(rows_from(region, stage, step), ROWS[stage])]

    def send_sums(region, stage, *slots):
        for slot in slots:
            step = STEP_OF[slot]
            pltpu.make_async_remote_copy(
                src_ref=sums_view(region, stage, GATE_OF[slot], step if slot < 4 else 2),
                dst_ref=region.boxes[stage].at[slot],
                send_sem=red_send.at[region.index * 3 + stage],
                recv_sem=red_recv.at[(region.index * 3 + stage) * 3 + max(slot - 3, 0)],
                device_id=near[region.axes[stage], step],
                device_id_type=MESH,
            ).start()

    def arrived(region, stage, group):
        box = region.boxes[stage]
        drain(box.at[pl.ds(0, 4)] if group == 0 else box.at[group + 3], red_recv.at[(region.index * 3 + stage) * 3 + group])

    def add_rows(target, *terms):
        count = target.shape[0] // 16
        together = min(count, 4)

        @pl.loop(0, count // together)
        def _(outer):
            for inner in range(together):
                at = pl.ds(multiple((outer * together + inner) * 16, 16), 16)
                value = target[at, :]
                for term in terms:
                    value = value + term[at, :]
                target[at, :] = value

    def terms(region, quarter):
        columns = pl.ds(multiple(region.offset + quarter * region.width, TILE), region.width)

        block = gathered[...].reshape(256, 256)
        for matrix in range(2):
            region.sums[matrix, quarter] = jnp.dot(
                block, weights[matrix, :, columns], preferred_element_type=jnp.float32
            ).astype(jnp.bfloat16)

    def task_first(region):
        wait_weights(region, 0)
        terms(region, quarters(region)[0])
        send_sums(region, 0, 4, 5)

    def task_second(region):
        for position, slot in ((1, 0), (2, 2), (3, None)):
            if region.wave == 0:
                wait_weights(region, position)
            terms(region, quarters(region)[position])
            if slot is not None:
                send_sums(region, 0, slot)

    def task_relay(stage):
        def run(region):
            for group, step, slot in ((1, 1, 1), (2, -1, 3)):
                arrived(region, stage, group)
                add_rows(sums_view(region, stage, group - 1, step), region.boxes[stage].at[group + 3])
                send_sums(region, stage, slot)

        return run

    def task_settle(stage):
        def run(region):
            arrived(region, stage, 0)
            box = region.boxes[stage]
            add_rows(sums_view(region, stage, 0, 0), box.at[1], box.at[2])
            add_rows(sums_view(region, stage, 1, 0), box.at[0], box.at[3])
            send_sums(region, stage + 1, 4, 5, 0, 2)

        return run

    def hidden_view(region, stage, step, part=None):
        size = ROWS[stage]
        if stage == 0:
            at, start = at_stage(region, 0, step), 0
            if part is None:
                return region.hidden.at[at]
        else:
            at, start = at_stage(region, 0), rows_from(region, stage, step)
        if part is not None:
            size //= 2
            start = start + part * size
        return region.hidden.at[at, pl.ds(start if isinstance(start, int) else multiple(start, 16), size)]

    def forwards(region, stage):
        return (2, 3) if stage < 2 else (2 + (region.color + region.wave) % 2,)

    def send_hidden(region, stage, *slots):
        for slot in slots:
            step = 1 if slot % 2 == 0 else -1
            view = hidden_view(region, stage, 0 if slot < 2 else -step, slot - 2 if slot >= 2 and stage < 2 else None)
            pltpu.make_async_remote_copy(
                src_ref=view,
                dst_ref=view,
                send_sem=all_send.at[region.index * 3 + stage],
                recv_sem=all_recv.at[(region.index * 3 + stage) * 2 + slot // 2],
                device_id=near[region.axes[stage], step],
                device_id_type=MESH,
            ).start()

    def hidden_rows(region, stage, count):
        if stage == 0 and count > 1:
            return region.hidden.at[pl.ds(0, count)]
        return region.hidden.at[0, pl.ds(0, ROWS[stage] * count)]

    def reached(region, stage, group):
        drain(hidden_rows(region, stage, 2 - group), all_recv.at[(region.index * 3 + stage) * 2 + group])

    def task_hidden(region):
        arrived(region, 2, 0)
        box = region.box3
        gate = sums_view(region, 2, 0, 0)[...].astype(jnp.float32)
        gate = gate + box[1].astype(jnp.float32) + box[2].astype(jnp.float32)
        up = sums_view(region, 2, 1, 0)[...].astype(jnp.float32)
        up = up + box[0].astype(jnp.float32) + box[3].astype(jnp.float32)
        hidden_view(region, 2, 0)[...] = (gate / (1.0 + jnp.exp(-gate)) * up).astype(jnp.bfloat16)
        send_hidden(region, 2, 0, 1)

    def task_forward(stage):
        def run(region):
            reached(region, stage, 0)
            send_hidden(region, stage, *forwards(region, stage))

        return run

    def task_gathered(stage):
        def run(region):
            reached(region, stage, 1)
            send_hidden(region, stage - 1, 0, 1)

        return run

    def project(region, quarter):
        columns = pl.ds(multiple(region.offset + quarter * region.width, TILE), region.width)
        total[...] += lax.dot_general(
            region.hidden[quarter], weights[2, :, columns], (((1,), (1,)), ((), ())), preferred_element_type=jnp.float32
        )

    def task_project(region):
        drain(weights.at[2, pl.ds(0, TILE), pl.ds(region.offset, SIDE * region.width)], d_own.at[region.index])
        drain(weights.at[2, pl.ds(0, TILE), pl.ds(region.offset, SIDE * region.width)], d_recv.at[region.index])
        reached(region, 0, 1)

        for quarter in range(SIDE):
            project(region, quarter)

    tasks = (
        task_first, task_second, task_relay(0), task_settle(0), task_relay(1), task_settle(1), task_relay(2),
        task_hidden, task_forward(2), task_gathered(2), task_forward(1), task_gathered(1), task_forward(0), task_project,
    )

    for region, position in weight_order():
        for matrix in range(2):
            term_weight(region, matrix, position, False).start()
    own_tokens = pltpu.make_async_copy(
        tokens.at[:, pl.ds(multiple(chip * 256, 256), 256)], gathered.at[col], exchange.at[4]
    )
    own_tokens.start()

    barrier = pltpu.get_barrier_semaphore()
    for step in range(1, cols):
        pl.semaphore_signal(barrier, inc=1, device_id=(row, peers[step]), device_id_type=MESH)
    for axis in (1, 2):
        for step in (1, -1):
            pl.semaphore_signal(barrier, inc=1, device_id=near[axis, step], device_id_type=MESH)
    pl.semaphore_wait(barrier, cols - 1 + 4)

    for step in range(1, cols):
        token_copy(step).start()
    for region, position in weight_order():
        for matrix in range(2):
            term_weight(region, matrix, position, True).start()
    for region in regions:
        down_weight(region, False).start()
        down_weight(region, True).start()

    total[...] = jnp.zeros_like(total)
    own_tokens.wait()
    drain(gathered.at[others], exchange.at[1])

    waves = len(WAVES)
    for tick in range(len(tasks) + LAG * (waves - 1)):
        for wave in range(waves):
            number = tick - LAG * wave
            if 0 <= number < len(tasks):
                for region in regions:
                    if region.wave == wave:
                        tasks[number](region)

    parts[...] = total[...].astype(jnp.bfloat16).reshape(cols, 16, 256)
    for step in range(1, cols):
        out_copy(step).start()
    inbox[col] = parts[col]
    drain(inbox.at[others], exchange.at[3])
    for block in range(cols // 2):
        out[:, block * 256 : (block + 1) * 256] = (
            inbox[2 * block].astype(jnp.float32) + inbox[2 * block + 1].astype(jnp.float32)
        ).astype(jnp.bfloat16)

    drain(gathered.at[others], exchange.at[0])
    drain(parts.at[others], exchange.at[2])
    for region in regions:
        columns = pl.ds(region.offset, SIDE * region.width)
        drain(weights.at[pl.ds(0, 2), pl.ds(0, TILE), columns], w_send.at[region.index])
        drain(weights.at[2, pl.ds(0, TILE), columns], d_send.at[region.index])
        for stage in range(3):
            drain(region.boxes[stage], red_send.at[region.index * 3 + stage])
            drain(hidden_rows(region, stage, 3), all_send.at[region.index * 3 + stage])


def on_device(tokens, gate_weight, up_weight, down_weight):
    batches, block, width = tokens.shape
    units = gate_weight.shape[1]
    half = units // 2
    regions = regions_of(half)
    count = len(regions)
    pieces = sum(region.pieces for region in regions)
    bf16 = jnp.bfloat16
    dma = pltpu.SemaphoreType.DMA

    scratch = [
        pltpu.VMEM((3, 256, half), bf16),
        pltpu.VMEM((16, 16, 256), bf16),
        pltpu.VMEM((16, 16, 256), bf16),
        pltpu.VMEM((16, 16, 256), bf16),
        pltpu.VMEM((256, 256), jnp.float32),
        dma((5,)),
        dma((pieces,)), dma((count,)), dma((pieces,)),
        dma((count,)), dma((count,)), dma((count,)),
        dma((count * 3,)), dma((count * 9,)), dma((count * 3,)), dma((count * 6,)),
    ]
    for region in regions:
        w = region.width
        scratch += [
            pltpu.VMEM((2, 4, 256, w), bf16),
            pltpu.VMEM((6, 256, w), bf16),
            pltpu.VMEM((6, 64, w), bf16),
            pltpu.VMEM((6, 16, w), bf16),
            pltpu.VMEM((4, 256, w), bf16),
        ]

    anywhere = pl.BlockSpec(memory_space=pl.ANY)
    out = pl.pallas_call(
        lambda *refs: kernel(regions, half, *refs),
        out_shape=jax.ShapeDtypeStruct((batches * block, width), bf16),
        in_specs=[anywhere] * 4,
        out_specs=pl.BlockSpec(memory_space=pltpu.VMEM),
        scratch_shapes=scratch,
        name="ffn",
        compiler_params=pltpu.CompilerParams(
            collective_id=0, has_side_effects=True, vmem_limit_bytes=67_000_000
        ),
    )(tokens.reshape(batches * block, width), gate_weight, up_weight, down_weight)
    return out.reshape(batches, block, width)


def solution(mesh):
    spread = P(("row", "col"), None)
    return jax.shard_map(
        on_device,
        mesh=mesh,
        in_specs=(P(None, "col", "row"), spread, spread, spread),
        out_specs=P(None, "col", "row"),
        check_vma=False,
    )
```

```python
import jax
import jax.numpy as jnp
from jax import lax
from jax.experimental import pallas as pl
from jax.experimental.pallas import tpu as pltpu
from jax.sharding import PartitionSpec as P

MESH = pl.DeviceIdType.MESH
SIDE = 4
TILE = 128
WAVES = ((3, 2, 2), (2, 3, 2), (2, 2, 2), (2, 2, 2))
GATE_OF = (1, 0, 0, 1, 0, 1)
STEP_OF = (1, 1, -1, -1, 1, -1)
LAG = 1
ROWS = (256, 64, 16)


def order_of(tasks):
    waves = len(WAVES)
    return [(wave, tick - LAG * wave) for tick in range(tasks + LAG * (waves - 1)) for wave in range(waves) if 0 <= tick - LAG * wave < tasks]


class Region:
    def __init__(self, wave, color, tiles, offset):
        self.wave, self.color, self.width, self.offset = wave, color, tiles * TILE, offset
        self.axes = tuple((color + i) % 3 for i in range(3))
        self.pieces = SIDE if wave == 0 else 1


def regions_of(units):
    regions, offset = [], 0
    for wave, tiles in enumerate(WAVES):
        for color, count in enumerate(tiles):
            if count == 0:
                continue
            region = Region(wave, color, count, offset)
            regions.append(region)
            offset += SIDE * region.width
    assert offset == units
    return regions


def multiple(value, of):
    return pl.multiple_of(value, of)


def kernel(regions, half, *refs):
    tokens, gate_hbm, up_hbm, down_hbm, out = refs[:5]
    weights, gathered, parts, inbox, total = refs[5:10]
    staged = refs[-1]
    exchange, w_own, w_send, w_recv, d_own, d_send, d_recv, red_send, red_recv, all_send, all_recv = refs[10:21]
    bufs = refs[21:]
    first = 0
    for index, region in enumerate(regions):
        region.index, region.first = index, first
        first += region.pieces
        region.sums, region.box1, region.box2, region.box3, region.hidden = bufs[5 * index : 5 * index + 5]
        region.boxes = (region.box1, region.box2, region.box3)

    row, col = lax.axis_index("row"), lax.axis_index("col")
    core = lax.rem(col, 2)
    chip = lax.div(col, 2)
    place = (lax.rem(chip, 4), lax.rem(row, 4), lax.div(row, 4) * 2 + lax.div(col, 8))
    cols = 16

    def device(x, y, z):
        return (lax.div(z, 2) * 4 + y, lax.rem(z, 2) * 8 + x * 2 + core)

    around = [[lax.rem(place[axis] + step, SIDE) for step in range(SIDE)] for axis in range(3)]
    near = {}
    for axis in range(3):
        for step in (1, 2, -1):
            at = list(place)
            at[axis] = around[axis][step]
            near[axis, step] = device(*at)
    partner = (row, chip * 2 + 1 - core)
    peers = [lax.rem(col + step, cols) for step in range(cols)]

    def drain(ref, sem):
        pltpu.make_async_copy(ref, ref, sem).wait()

    hbm = (gate_hbm, up_hbm, down_hbm)

    def weight_columns(region, quarter):
        if quarter is None:
            return region.offset, SIDE * region.width
        return region.offset + quarter * region.width, region.width

    def weight_copy(region, matrix, quarter, sems, remote):
        start, size = weight_columns(region, quarter)
        rows = pl.ds(multiple(core * TILE, TILE), TILE)
        here = weights.at[matrix, rows, pl.ds(multiple(start, TILE), size)]
        which = 1 - core if remote else core
        source = hbm[matrix].at[:, pl.ds(multiple(which * half + start, TILE), size)]
        own, send, recv = sems
        if not remote:
            return pltpu.make_async_copy(source, here, own)
        return pltpu.make_async_remote_copy(
            src_ref=source, dst_ref=here, send_sem=send, recv_sem=recv, device_id=partner, device_id_type=MESH
        )

    def quarters(region):
        return [around[region.axes[0]][step] for step in (2, 1, -1, 0)]

    def term_weight(region, matrix, position, remote):
        quarter = quarters(region)[position] if region.wave == 0 else None
        index = region.first + position
        sems = (w_own.at[index], w_send.at[region.index], w_recv.at[index])
        return weight_copy(region, matrix, quarter, sems, remote)

    def wait_weights(region, position):
        start, size = weight_columns(region, quarters(region)[position] if region.wave == 0 else None)
        both = weights.at[pl.ds(0, 2), pl.ds(0, TILE), pl.ds(multiple(start, TILE), size)]
        drain(both, w_own.at[region.first + position])
        drain(both, w_recv.at[region.first + position])

    def down_weight(region, remote):
        index = region.index
        return weight_copy(region, 2, None, (d_own.at[index], d_send.at[index], d_recv.at[index]), remote)

    def weight_order():
        for position in range(4):
            for region in regions:
                if region.wave == 0:
                    yield region, position
        for region in regions:
            if region.wave > 0:
                yield region, 0

    def token_copy(step):
        to = peers[step]
        return pltpu.make_async_remote_copy(
            src_ref=staged.at[lax.div(to, 2)],
            dst_ref=gathered.at[col],
            send_sem=exchange.at[0],
            recv_sem=exchange.at[1],
            device_id=(row, to),
            device_id_type=MESH,
        )

    def out_copy(step):
        to = peers[step]
        return pltpu.make_async_remote_copy(
            src_ref=parts.at[to],
            dst_ref=inbox.at[col],
            send_sem=exchange.at[2],
            recv_sem=exchange.at[3],
            device_id=(row, to),
            device_id_type=MESH,
        )

    others = pl.ds(0, cols - 1)

    def at_stage(region, stage, step=0):
        return around[region.axes[stage]][step]

    def rows_from(region, stage, step):
        if stage == 1:
            return multiple(at_stage(region, 1, step) * 64, 64)
        return multiple(at_stage(region, 1) * 64 + at_stage(region, 2, step) * 16, 16)

    def sums_view(region, stage, matrix, step):
        if stage == 0:
            return region.sums.at[matrix, at_stage(region, 0, step)]
        return region.sums.at[matrix, at_stage(region, 0), pl.ds(rows_from(region, stage, step), ROWS[stage])]

    def send_sums(region, stage, *slots):
        for slot in slots:
            step = STEP_OF[slot]
            pltpu.make_async_remote_copy(
                src_ref=sums_view(region, stage, GATE_OF[slot], step if slot < 4 else 2),
                dst_ref=region.boxes[stage].at[slot],
                send_sem=red_send.at[region.index * 3 + stage],
                recv_sem=red_recv.at[region.index * 7 + stage * 3 + max(slot - 3, 0)],
                device_id=near[region.axes[stage], step],
                device_id_type=MESH,
            ).start()

    def send_last(region):
        first = at_stage(region, 0)
        for slot, step in enumerate((2, 1, -1)):
            rows = pl.ds(rows_from(region, 2, step), ROWS[2])
            pltpu.make_async_remote_copy(
                src_ref=region.sums.at[:, first, rows],
                dst_ref=region.box3.at[slot],
                send_sem=red_send.at[region.index * 3 + 2],
                recv_sem=red_recv.at[region.index * 7 + 6],
                device_id=near[region.axes[2], step],
                device_id_type=MESH,
            ).start()

    def arrived(region, stage, group):
        box = region.boxes[stage]
        drain(box.at[pl.ds(0, 4)] if group == 0 else box.at[group + 3], red_recv.at[region.index * 7 + stage * 3 + group])

    def add_rows(target, *terms):
        count = target.shape[0] // 16
        together = min(count, 4)

        @pl.loop(0, count // together)
        def _(outer):
            for inner in range(together):
                at = pl.ds(multiple((outer * together + inner) * 16, 16), 16)
                value = target[at, :]
                for term in terms:
                    value = value + term[at, :]
                target[at, :] = value

    def terms(region, quarter):
        columns = pl.ds(multiple(region.offset + quarter * region.width, TILE), region.width)

        block = gathered[...].reshape(256, 256)
        for matrix in range(2):
            region.sums[matrix, quarter] = jnp.dot(
                block, weights[matrix, :, columns], preferred_element_type=jnp.float32
            ).astype(jnp.bfloat16)

    def task_first(region):
        wait_weights(region, 0)
        terms(region, quarters(region)[0])
        send_sums(region, 0, 4, 5)

    def task_second(region):
        for position, slot in ((1, 0), (2, 2), (3, None)):
            if region.wave == 0:
                wait_weights(region, position)
            terms(region, quarters(region)[position])
            if slot is not None:
                send_sums(region, 0, slot)

    def task_relay(stage):
        def run(region):
            for group, step, slot in ((1, 1, 1), (2, -1, 3)):
                arrived(region, stage, group)
                add_rows(sums_view(region, stage, group - 1, step), region.boxes[stage].at[group + 3])
                send_sums(region, stage, slot)

        return run

    def task_settle(stage):
        def run(region):
            arrived(region, stage, 0)
            box = region.boxes[stage]
            add_rows(sums_view(region, stage, 0, 0), box.at[1], box.at[2])
            add_rows(sums_view(region, stage, 1, 0), box.at[0], box.at[3])
            if stage == 0:
                send_sums(region, 1, 4, 5, 0, 2)
            else:
                send_last(region)

        return run

    def hidden_view(region, stage, step, part=None):
        size = ROWS[stage]
        if stage == 0:
            at, start = at_stage(region, 0, step), 0
            if part is None:
                return region.hidden.at[at]
        else:
            at, start = at_stage(region, 0), rows_from(region, stage, step)
        if part is not None:
            size //= 2
            start = start + part * size
        return region.hidden.at[at, pl.ds(start if isinstance(start, int) else multiple(start, 16), size)]

    def send_hidden(region, stage, *slots):
        for slot in slots:
            step = 1 if slot % 2 == 0 else -1
            view = hidden_view(region, stage, 0 if slot < 2 else -step, slot - 2 if slot >= 2 else None)
            pltpu.make_async_remote_copy(
                src_ref=view,
                dst_ref=view,
                send_sem=all_send.at[region.index * 3 + stage],
                recv_sem=all_recv.at[(region.index * 3 + stage) * 2 + slot // 2],
                device_id=near[region.axes[stage], step],
                device_id_type=MESH,
            ).start()

    def send_first(region):
        view = hidden_view(region, 2, 0)
        for step in (2, 1, -1):
            pltpu.make_async_remote_copy(
                src_ref=view,
                dst_ref=view,
                send_sem=all_send.at[region.index * 3 + 2],
                recv_sem=all_recv.at[(region.index * 3 + 2) * 2],
                device_id=near[region.axes[2], step],
                device_id_type=MESH,
            ).start()

    def hidden_rows(region, stage, count):
        if stage == 0 and count > 1:
            return region.hidden.at[pl.ds(0, count)]
        return region.hidden.at[0, pl.ds(0, ROWS[stage] * count)]

    def reached(region, stage, group):
        drain(hidden_rows(region, stage, 2 - group), all_recv.at[(region.index * 3 + stage) * 2 + group])

    def task_hidden(region):
        box = region.box3
        drain(box, red_recv.at[region.index * 7 + 6])
        at, rows = at_stage(region, 0), pl.ds(rows_from(region, 2, 0), ROWS[2])
        gate, up = (
            region.sums[matrix, at, rows].astype(jnp.float32)
            + box[0, matrix].astype(jnp.float32)
            + box[1, matrix].astype(jnp.float32)
            + box[2, matrix].astype(jnp.float32)
            for matrix in range(2)
        )
        hidden_view(region, 2, 0)[...] = (gate / (1.0 + jnp.exp(-gate)) * up).astype(jnp.bfloat16)
        send_first(region)

    def task_forward(stage):
        def run(region):
            reached(region, stage, 0)
            send_hidden(region, stage, 2, 3)

        return run

    def task_gathered(stage):
        def run(region):
            if stage == 2:
                drain(hidden_rows(region, 2, 3), all_recv.at[(region.index * 3 + 2) * 2])
            else:
                reached(region, stage, 1)
            send_hidden(region, stage - 1, 0, 1)

        return run

    def project(region, quarter):
        columns = pl.ds(multiple(region.offset + quarter * region.width, TILE), region.width)
        total[...] += lax.dot_general(
            region.hidden[quarter], weights[2, :, columns], (((1,), (1,)), ((), ())), preferred_element_type=jnp.float32
        )

    def task_project(region):
        drain(weights.at[2, pl.ds(0, TILE), pl.ds(region.offset, SIDE * region.width)], d_own.at[region.index])
        drain(weights.at[2, pl.ds(0, TILE), pl.ds(region.offset, SIDE * region.width)], d_recv.at[region.index])
        reached(region, 0, 1)

        for quarter in range(SIDE):
            project(region, quarter)

    tasks = (
        task_first, task_second, task_relay(0), task_settle(0), task_relay(1), task_settle(1),
        task_hidden, task_gathered(2), task_forward(1), task_gathered(1), task_forward(0), task_project,
    )

    for block in range(cols // 2):
        pltpu.make_async_copy(tokens.at[:, pl.ds(block * 256, 256)], staged.at[block], exchange.at[4]).start()
    for region, position in weight_order():
        for matrix in range(2):
            term_weight(region, matrix, position, False).start()
    drain(staged, exchange.at[4])

    barrier = pltpu.get_barrier_semaphore()
    for step in range(1, cols):
        pl.semaphore_signal(barrier, inc=1, device_id=(row, peers[step]), device_id_type=MESH)
    for axis in (1, 2):
        for step in (1, 2, -1):
            pl.semaphore_signal(barrier, inc=1, device_id=near[axis, step], device_id_type=MESH)
    pl.semaphore_wait(barrier, cols - 1 + 6)

    for step in range(1, cols):
        token_copy(step).start()
    for region, position in weight_order():
        for matrix in range(2):
            term_weight(region, matrix, position, True).start()
    for region in regions:
        down_weight(region, False).start()
        down_weight(region, True).start()

    total[...] = jnp.zeros_like(total)
    gathered[col] = staged[chip]
    drain(gathered.at[others], exchange.at[1])

    for wave, number in order_of(len(tasks)):
        for region in regions:
            if region.wave == wave:
                tasks[number](region)

    parts[...] = total[...].astype(jnp.bfloat16).reshape(cols, 16, 256)
    for step in range(1, cols):
        out_copy(step).start()
    inbox[col] = parts[col]
    drain(inbox.at[others], exchange.at[3])
    for block in range(cols // 2):
        out[:, block * 256 : (block + 1) * 256] = (
            inbox[2 * block].astype(jnp.float32) + inbox[2 * block + 1].astype(jnp.float32)
        ).astype(jnp.bfloat16)

    drain(gathered.at[others], exchange.at[0])
    drain(parts.at[others], exchange.at[2])
    for region in regions:
        columns = pl.ds(region.offset, SIDE * region.width)
        drain(weights.at[pl.ds(0, 2), pl.ds(0, TILE), columns], w_send.at[region.index])
        drain(weights.at[2, pl.ds(0, TILE), columns], d_send.at[region.index])
        for stage in range(3):
            drain(region.boxes[stage], red_send.at[region.index * 3 + stage])
            drain(hidden_rows(region, stage, 3), all_send.at[region.index * 3 + stage])


def on_device(tokens, gate_weight, up_weight, down_weight):
    batches, block, width = tokens.shape
    units = gate_weight.shape[1]
    half = units // 2
    regions = regions_of(half)
    count = len(regions)
    pieces = sum(region.pieces for region in regions)
    bf16 = jnp.bfloat16
    dma = pltpu.SemaphoreType.DMA

    scratch = [
        pltpu.VMEM((3, 256, half), bf16),
        pltpu.VMEM((16, 16, 256), bf16),
        pltpu.VMEM((16, 16, 256), bf16),
        pltpu.VMEM((16, 16, 256), bf16),
        pltpu.VMEM((256, 256), jnp.float32),
        dma((5,)),
        dma((pieces,)), dma((count,)), dma((pieces,)),
        dma((count,)), dma((count,)), dma((count,)),
        dma((count * 3,)), dma((count * 7,)), dma((count * 3,)), dma((count * 6,)),
    ]
    for region in regions:
        w = region.width
        scratch += [
            pltpu.VMEM((2, 4, 256, w), bf16),
            pltpu.VMEM((6, 256, w), bf16),
            pltpu.VMEM((6, 64, w), bf16),
            pltpu.VMEM((3, 2, 16, w), bf16),
            pltpu.VMEM((4, 256, w), bf16),
        ]

    scratch.append(pltpu.VMEM((8, 16, 256), bf16))
    anywhere = pl.BlockSpec(memory_space=pl.ANY)
    out = pl.pallas_call(
        lambda *refs: kernel(regions, half, *refs),
        out_shape=jax.ShapeDtypeStruct((batches * block, width), bf16),
        in_specs=[anywhere] * 4,
        out_specs=pl.BlockSpec(memory_space=pltpu.VMEM),
        scratch_shapes=scratch,
        name="ffn",
        compiler_params=pltpu.CompilerParams(
            collective_id=0, has_side_effects=True, vmem_limit_bytes=67_000_000
        ),
    )(tokens.reshape(batches * block, width), gate_weight, up_weight, down_weight)
    return out.reshape(batches, block, width)


def solution(mesh):
    spread = P(("row", "col"), None)
    return jax.shard_map(
        on_device,
        mesh=mesh,
        in_specs=(P(None, "col", "row"), spread, spread, spread),
        out_specs=P(None, "col", "row"),
        check_vma=False,
    )
```

```python
import jax
import jax.numpy as jnp
from jax import lax
from jax.experimental import pallas as pl
from jax.experimental.pallas import tpu as pltpu
from jax.sharding import PartitionSpec as P

MESH = pl.DeviceIdType.MESH
SIDE = 4
TILE = 128
WAVES = ((1, 1, 1), (2, 2, 2), (2, 2, 2), (2, 2, 2), (2, 2, 1))
GATE_OF = (1, 0, 0, 1, 0, 1)
STEP_OF = (1, 1, -1, -1, 1, -1)
ORDER = (0, 0, 1, 1, 0, 4, 2, 0, 1, 3, 2, 0, 1, 2, 3, 0, 1, 3, 2, 1, 4, 0, 2, 3, 4, 3, 0, 1, 2, 4, 0, 3, 1, 2, 4, 0, 1, 3, 4, 2, 1, 4, 3, 2, 0, 1, 3, 4, 2, 4, 3, 4, 3, 2, 0, 1, 4, 3, 2, 4)
ROWS = (256, 64, 16)


def order_of(tasks):
    done, order = [0] * len(WAVES), []
    for wave in ORDER:
        order.append((wave, done[wave]))
        done[wave] += 1
    assert all(count == tasks for count in done)
    return order


class Region:
    def __init__(self, wave, color, tiles, offset):
        self.wave, self.color, self.width, self.offset = wave, color, tiles * TILE, offset
        self.axes = tuple((color + i) % 3 for i in range(3))
        self.pieces = SIDE if wave == 0 else 1


def regions_of(units):
    regions, offset = [], 0
    for wave, tiles in enumerate(WAVES):
        for color, count in enumerate(tiles):
            if count == 0:
                continue
            region = Region(wave, color, count, offset)
            regions.append(region)
            offset += SIDE * region.width
    assert offset == units
    return regions


def multiple(value, of):
    return pl.multiple_of(value, of)


def kernel(regions, half, *refs):
    tokens, gate_hbm, up_hbm, down_hbm, out = refs[:5]
    weights, gathered, parts, inbox, total = refs[5:10]
    staged = refs[-1]
    exchange, w_own, w_send, w_recv, d_own, d_send, d_recv, red_send, red_recv, all_send, all_recv = refs[10:21]
    bufs = refs[21:]
    first = 0
    for index, region in enumerate(regions):
        region.index, region.first = index, first
        first += region.pieces
        region.sums, region.box1, region.box2, region.box3, region.hidden = bufs[5 * index : 5 * index + 5]
        region.boxes = (region.box1, region.box2, region.box3)

    row, col = lax.axis_index("row"), lax.axis_index("col")
    core = lax.rem(col, 2)
    chip = lax.div(col, 2)
    place = (lax.rem(chip, 4), lax.rem(row, 4), lax.div(row, 4) * 2 + lax.div(col, 8))
    cols = 16

    def device(x, y, z):
        return (lax.div(z, 2) * 4 + y, lax.rem(z, 2) * 8 + x * 2 + core)

    around = [[lax.rem(place[axis] + step, SIDE) for step in range(SIDE)] for axis in range(3)]
    near = {}
    for axis in range(3):
        for step in (1, 2, -1):
            at = list(place)
            at[axis] = around[axis][step]
            near[axis, step] = device(*at)
    partner = (row, chip * 2 + 1 - core)
    peers = [lax.rem(col + step, cols) for step in range(cols)]

    def drain(ref, sem):
        pltpu.make_async_copy(ref, ref, sem).wait()

    hbm = (gate_hbm, up_hbm, down_hbm)

    def weight_columns(region, quarter):
        if quarter is None:
            return region.offset, SIDE * region.width
        return region.offset + quarter * region.width, region.width

    def weight_copy(region, matrix, quarter, sems, remote):
        start, size = weight_columns(region, quarter)
        rows = pl.ds(multiple(core * TILE, TILE), TILE)
        here = weights.at[matrix, rows, pl.ds(multiple(start, TILE), size)]
        which = 1 - core if remote else core
        source = hbm[matrix].at[:, pl.ds(multiple(which * half + start, TILE), size)]
        own, send, recv = sems
        if not remote:
            return pltpu.make_async_copy(source, here, own)
        return pltpu.make_async_remote_copy(
            src_ref=source, dst_ref=here, send_sem=send, recv_sem=recv, device_id=partner, device_id_type=MESH
        )

    def quarters(region):
        return [around[region.axes[0]][step] for step in (2, 1, -1, 0)]

    def term_weight(region, matrix, position, remote):
        quarter = quarters(region)[position] if region.wave == 0 else None
        index = region.first + position
        sems = (w_own.at[index], w_send.at[region.index], w_recv.at[index])
        return weight_copy(region, matrix, quarter, sems, remote)

    def wait_weights(region, position):
        start, size = weight_columns(region, quarters(region)[position] if region.wave == 0 else None)
        both = weights.at[pl.ds(0, 2), pl.ds(0, TILE), pl.ds(multiple(start, TILE), size)]
        drain(both, w_own.at[region.first + position])
        drain(both, w_recv.at[region.first + position])

    def down_weight(region, remote):
        index = region.index
        return weight_copy(region, 2, None, (d_own.at[index], d_send.at[index], d_recv.at[index]), remote)

    def weight_order():
        for position in range(4):
            for region in regions:
                if region.wave == 0:
                    yield region, position
        for region in regions:
            if region.wave > 0:
                yield region, 0

    def token_copy(step):
        to = peers[step]
        return pltpu.make_async_remote_copy(
            src_ref=staged.at[lax.div(to, 2)],
            dst_ref=gathered.at[col],
            send_sem=exchange.at[0],
            recv_sem=exchange.at[1],
            device_id=(row, to),
            device_id_type=MESH,
        )

    def out_copy(step):
        to = peers[step]
        return pltpu.make_async_remote_copy(
            src_ref=parts.at[to],
            dst_ref=inbox.at[col],
            send_sem=exchange.at[2],
            recv_sem=exchange.at[3],
            device_id=(row, to),
            device_id_type=MESH,
        )

    others = pl.ds(0, cols - 1)

    def at_stage(region, stage, step=0):
        return around[region.axes[stage]][step]

    def rows_from(region, stage, step):
        if stage == 1:
            return multiple(at_stage(region, 1, step) * 64, 64)
        return multiple(at_stage(region, 1) * 64 + at_stage(region, 2, step) * 16, 16)

    def sums_view(region, stage, matrix, step):
        if stage == 0:
            return region.sums.at[matrix, at_stage(region, 0, step)]
        return region.sums.at[matrix, at_stage(region, 0), pl.ds(rows_from(region, stage, step), ROWS[stage])]

    def send_sums(region, stage, *slots):
        for slot in slots:
            step = STEP_OF[slot]
            pltpu.make_async_remote_copy(
                src_ref=sums_view(region, stage, GATE_OF[slot], step if slot < 4 else 2),
                dst_ref=region.boxes[stage].at[slot],
                send_sem=red_send.at[region.index * 3 + stage],
                recv_sem=red_recv.at[region.index * 7 + stage * 3 + max(slot - 3, 0)],
                device_id=near[region.axes[stage], step],
                device_id_type=MESH,
            ).start()

    def send_last(region):
        first = at_stage(region, 0)
        for slot, step in enumerate((2, 1, -1)):
            rows = pl.ds(rows_from(region, 2, step), ROWS[2])
            pltpu.make_async_remote_copy(
                src_ref=region.sums.at[:, first, rows],
                dst_ref=region.box3.at[slot],
                send_sem=red_send.at[region.index * 3 + 2],
                recv_sem=red_recv.at[region.index * 7 + 6],
                device_id=near[region.axes[2], step],
                device_id_type=MESH,
            ).start()

    def arrived(region, stage, group):
        box = region.boxes[stage]
        drain(box.at[pl.ds(0, 4)] if group == 0 else box.at[group + 3], red_recv.at[region.index * 7 + stage * 3 + group])

    def add_rows(target, *terms):
        count = target.shape[0] // 16
        together = min(count, 4)

        @pl.loop(0, count // together)
        def _(outer):
            for inner in range(together):
                at = pl.ds(multiple((outer * together + inner) * 16, 16), 16)
                value = target[at, :]
                for term in terms:
                    value = value + term[at, :]
                target[at, :] = value

    def terms(region, quarter):
        columns = pl.ds(multiple(region.offset + quarter * region.width, TILE), region.width)

        block = gathered[...].reshape(256, 256)
        for matrix in range(2):
            region.sums[matrix, quarter] = jnp.dot(
                block, weights[matrix, :, columns], preferred_element_type=jnp.float32
            ).astype(jnp.bfloat16)

    def task_first(region):
        wait_weights(region, 0)
        terms(region, quarters(region)[0])
        send_sums(region, 0, 4, 5)

    def task_second(region):
        for position, slot in ((1, 0), (2, 2), (3, None)):
            if region.wave == 0:
                wait_weights(region, position)
            terms(region, quarters(region)[position])
            if slot is not None:
                send_sums(region, 0, slot)

    def task_relay(stage):
        def run(region):
            for group, step, slot in ((1, 1, 1), (2, -1, 3)):
                arrived(region, stage, group)
                add_rows(sums_view(region, stage, group - 1, step), region.boxes[stage].at[group + 3])
                send_sums(region, stage, slot)

        return run

    def task_settle(stage):
        def run(region):
            arrived(region, stage, 0)
            box = region.boxes[stage]
            add_rows(sums_view(region, stage, 0, 0), box.at[1], box.at[2])
            add_rows(sums_view(region, stage, 1, 0), box.at[0], box.at[3])
            if stage == 0:
                send_sums(region, 1, 4, 5, 0, 2)
            else:
                send_last(region)

        return run

    def hidden_view(region, stage, step, part=None):
        size = ROWS[stage]
        if stage == 0:
            at, start = at_stage(region, 0, step), 0
            if part is None:
                return region.hidden.at[at]
        else:
            at, start = at_stage(region, 0), rows_from(region, stage, step)
        if part is not None:
            size //= 2
            start = start + part * size
        return region.hidden.at[at, pl.ds(start if isinstance(start, int) else multiple(start, 16), size)]

    def send_hidden(region, stage, *slots):
        for slot in slots:
            step = 1 if slot % 2 == 0 else -1
            view = hidden_view(region, stage, 0 if slot < 2 else -step, slot - 2 if slot >= 2 else None)
            pltpu.make_async_remote_copy(
                src_ref=view,
                dst_ref=view,
                send_sem=all_send.at[region.index * 3 + stage],
                recv_sem=all_recv.at[(region.index * 3 + stage) * 2 + slot // 2],
                device_id=near[region.axes[stage], step],
                device_id_type=MESH,
            ).start()

    def send_first(region):
        view = hidden_view(region, 2, 0)
        for step in (2, 1, -1):
            pltpu.make_async_remote_copy(
                src_ref=view,
                dst_ref=view,
                send_sem=all_send.at[region.index * 3 + 2],
                recv_sem=all_recv.at[(region.index * 3 + 2) * 2],
                device_id=near[region.axes[2], step],
                device_id_type=MESH,
            ).start()

    def hidden_rows(region, stage, count):
        if stage == 0 and count > 1:
            return region.hidden.at[pl.ds(0, count)]
        return region.hidden.at[0, pl.ds(0, ROWS[stage] * count)]

    def reached(region, stage, group):
        drain(hidden_rows(region, stage, 2 - group), all_recv.at[(region.index * 3 + stage) * 2 + group])

    def task_hidden(region):
        box = region.box3
        drain(box, red_recv.at[region.index * 7 + 6])
        at, rows = at_stage(region, 0), pl.ds(rows_from(region, 2, 0), ROWS[2])
        gate, up = (
            region.sums[matrix, at, rows].astype(jnp.float32)
            + box[0, matrix].astype(jnp.float32)
            + box[1, matrix].astype(jnp.float32)
            + box[2, matrix].astype(jnp.float32)
            for matrix in range(2)
        )
        hidden_view(region, 2, 0)[...] = (gate / (1.0 + jnp.exp(-gate)) * up).astype(jnp.bfloat16)
        send_first(region)

    def task_forward(stage):
        def run(region):
            reached(region, stage, 0)
            send_hidden(region, stage, 2, 3)
            if stage == 0:
                columns = pl.ds(region.offset, SIDE * region.width)
                drain(weights.at[2, pl.ds(0, TILE), columns], d_own.at[region.index])
                drain(weights.at[2, pl.ds(0, TILE), columns], d_recv.at[region.index])
                for step in (0, 1, -1):
                    project(region, at_stage(region, 0, step))

        return run

    def task_gathered(stage):
        def run(region):
            if stage == 2:
                drain(hidden_rows(region, 2, 3), all_recv.at[(region.index * 3 + 2) * 2])
            else:
                reached(region, stage, 1)
            send_hidden(region, stage - 1, 0, 1)

        return run

    def project(region, quarter):
        columns = pl.ds(multiple(region.offset + quarter * region.width, TILE), region.width)
        total[...] += lax.dot_general(
            region.hidden[quarter], weights[2, :, columns], (((1,), (1,)), ((), ())), preferred_element_type=jnp.float32
        )

    def task_project(region):
        reached(region, 0, 1)
        project(region, at_stage(region, 0, 2))

    tasks = (
        task_first, task_second, task_relay(0), task_settle(0), task_relay(1), task_settle(1),
        task_hidden, task_gathered(2), task_forward(1), task_gathered(1), task_forward(0), task_project,
    )

    for block in range(cols // 2):
        pltpu.make_async_copy(tokens.at[:, pl.ds(block * 256, 256)], staged.at[block], exchange.at[4]).start()
    for region, position in weight_order():
        for matrix in range(2):
            term_weight(region, matrix, position, False).start()
    drain(staged, exchange.at[4])

    barrier = pltpu.get_barrier_semaphore()
    for step in range(1, cols):
        pl.semaphore_signal(barrier, inc=1, device_id=(row, peers[step]), device_id_type=MESH)
    for axis in (1, 2):
        for step in (1, 2, -1):
            pl.semaphore_signal(barrier, inc=1, device_id=near[axis, step], device_id_type=MESH)
    pl.semaphore_wait(barrier, cols - 1 + 6)

    for step in range(1, cols):
        token_copy(step).start()
    for region, position in weight_order():
        for matrix in range(2):
            term_weight(region, matrix, position, True).start()
    for region in regions:
        down_weight(region, False).start()
        down_weight(region, True).start()

    total[...] = jnp.zeros_like(total)
    gathered[col] = staged[chip]
    drain(gathered.at[others], exchange.at[1])

    for wave, number in order_of(len(tasks)):
        for region in regions:
            if region.wave == wave:
                tasks[number](region)

    parts[...] = total[...].astype(jnp.bfloat16).reshape(cols, 16, 256)
    for step in range(1, cols):
        out_copy(step).start()
    inbox[col] = parts[col]
    drain(inbox.at[others], exchange.at[3])
    for block in range(cols // 2):
        out[:, block * 256 : (block + 1) * 256] = (
            inbox[2 * block].astype(jnp.float32) + inbox[2 * block + 1].astype(jnp.float32)
        ).astype(jnp.bfloat16)

    drain(gathered.at[others], exchange.at[0])
    drain(parts.at[others], exchange.at[2])
    for region in regions:
        columns = pl.ds(region.offset, SIDE * region.width)
        drain(weights.at[pl.ds(0, 2), pl.ds(0, TILE), columns], w_send.at[region.index])
        drain(weights.at[2, pl.ds(0, TILE), columns], d_send.at[region.index])
        for stage in range(3):
            drain(region.boxes[stage], red_send.at[region.index * 3 + stage])
            drain(hidden_rows(region, stage, 3), all_send.at[region.index * 3 + stage])


def on_device(tokens, gate_weight, up_weight, down_weight):
    batches, block, width = tokens.shape
    units = gate_weight.shape[1]
    half = units // 2
    regions = regions_of(half)
    count = len(regions)
    pieces = sum(region.pieces for region in regions)
    bf16 = jnp.bfloat16
    dma = pltpu.SemaphoreType.DMA

    scratch = [
        pltpu.VMEM((3, 256, half), bf16),
        pltpu.VMEM((16, 16, 256), bf16),
        pltpu.VMEM((16, 16, 256), bf16),
        pltpu.VMEM((16, 16, 256), bf16),
        pltpu.VMEM((256, 256), jnp.float32),
        dma((5,)),
        dma((pieces,)), dma((count,)), dma((pieces,)),
        dma((count,)), dma((count,)), dma((count,)),
        dma((count * 3,)), dma((count * 7,)), dma((count * 3,)), dma((count * 6,)),
    ]
    for region in regions:
        w = region.width
        scratch += [
            pltpu.VMEM((2, 4, 256, w), bf16),
            pltpu.VMEM((6, 256, w), bf16),
            pltpu.VMEM((6, 64, w), bf16),
            pltpu.VMEM((3, 2, 16, w), bf16),
            pltpu.VMEM((4, 256, w), bf16),
        ]

    scratch.append(pltpu.VMEM((8, 16, 256), bf16))
    anywhere = pl.BlockSpec(memory_space=pl.ANY)
    out = pl.pallas_call(
        lambda *refs: kernel(regions, half, *refs),
        out_shape=jax.ShapeDtypeStruct((batches * block, width), bf16),
        in_specs=[anywhere] * 4,
        out_specs=pl.BlockSpec(memory_space=pltpu.VMEM),
        scratch_shapes=scratch,
        name="ffn",
        compiler_params=pltpu.CompilerParams(
            collective_id=0, has_side_effects=True, vmem_limit_bytes=67_000_000
        ),
    )(tokens.reshape(batches * block, width), gate_weight, up_weight, down_weight)
    return out.reshape(batches, block, width)


def solution(mesh):
    spread = P(("row", "col"), None)
    return jax.shard_map(
        on_device,
        mesh=mesh,
        in_specs=(P(None, "col", "row"), spread, spread, spread),
        out_specs=P(None, "col", "row"),
        check_vma=False,
    )
```

```python
import jax
import jax.numpy as jnp
from jax import lax
from jax.experimental import pallas as pl
from jax.experimental.pallas import tpu as pltpu
from jax.sharding import PartitionSpec as P

MESH = pl.DeviceIdType.MESH
SIDE = 4
TILE = 128
WAVES = ((1, 1, 1), (2, 2, 2), (2, 2, 2), (2, 2, 2), (2, 2, 1))
GATE_OF = (1, 0, 0, 1, 0, 1)
STEP_OF = (1, 1, -1, -1, 1, -1)
ORDER = (0, 0, 1, 1, 0, 4, 2, 0, 1, 3, 2, 0, 1, 2, 3, 0, 1, 3, 2, 1, 4, 0, 2, 3, 4, 3, 0, 1, 2, 4, 0, 3, 1, 2, 4, 0, 1, 3, 4, 2, 1, 4, 3, 2, 0, 1, 3, 4, 2, 4, 3, 4, 3, 2, 0, 1, 4, 3, 2, 4)
ROWS = (256, 64, 16)


def order_of(tasks):
    done, order = [0] * len(WAVES), []
    for wave in ORDER:
        order.append((wave, done[wave]))
        done[wave] += 1
    assert all(count == tasks for count in done)
    return order


class Region:
    def __init__(self, wave, color, tiles, offset):
        self.wave, self.color, self.width, self.offset = wave, color, tiles * TILE, offset
        self.axes = tuple((color + i) % 3 for i in range(3))
        self.pieces = SIDE if wave == 0 else 1


def regions_of(units):
    regions, offset = [], 0
    for wave, tiles in enumerate(WAVES):
        for color, count in enumerate(tiles):
            if count == 0:
                continue
            region = Region(wave, color, count, offset)
            regions.append(region)
            offset += SIDE * region.width
    assert offset == units
    return regions


def multiple(value, of):
    return pl.multiple_of(value, of)


def kernel(regions, half, *refs):
    tokens, gate_hbm, up_hbm, down_hbm, out = refs[:5]
    weights, gathered, parts, inbox, total = refs[5:10]
    staged = refs[-1]
    exchange, shared, w_own, w_recv, red_recv, all_recv = refs[10:16]
    bufs = refs[16:]
    first = 0
    for index, region in enumerate(regions):
        region.index, region.first = index, first
        first += region.pieces
        region.sums, region.box1, region.box2, region.box3, region.hidden = bufs[5 * index : 5 * index + 5]
        region.boxes = (region.box1, region.box2, region.box3)

    row, col = lax.axis_index("row"), lax.axis_index("col")
    core = lax.rem(col, 2)
    chip = lax.div(col, 2)
    place = (lax.rem(chip, 4), lax.rem(row, 4), lax.div(row, 4) * 2 + lax.div(col, 8))
    cols = 16

    def device(x, y, z):
        return (lax.div(z, 2) * 4 + y, lax.rem(z, 2) * 8 + x * 2 + core)

    around = [[lax.rem(place[axis] + step, SIDE) for step in range(SIDE)] for axis in range(3)]
    near = {}
    for axis in range(3):
        for step in (1, 2, -1):
            at = list(place)
            at[axis] = around[axis][step]
            near[axis, step] = device(*at)
    partner = (row, chip * 2 + 1 - core)
    peers = [lax.rem(col + step, cols) for step in range(cols)]

    def drain(ref, sem):
        pltpu.make_async_copy(ref, ref, sem).wait()

    hbm = (gate_hbm, up_hbm, down_hbm)

    def weight_columns(region, quarter):
        if quarter is None:
            return region.offset, SIDE * region.width
        return region.offset + quarter * region.width, region.width

    def weight_copy(region, matrix, quarter, sems, remote):
        start, size = weight_columns(region, quarter)
        rows = pl.ds(multiple(core * TILE, TILE), TILE)
        here = weights.at[matrix, rows, pl.ds(multiple(start, TILE), size)]
        which = 1 - core if remote else core
        source = hbm[matrix].at[:, pl.ds(multiple(which * half + start, TILE), size)]
        own, send, recv = sems
        if not remote:
            return pltpu.make_async_copy(source, here, own)
        return pltpu.make_async_remote_copy(
            src_ref=source, dst_ref=here, send_sem=send, recv_sem=recv, device_id=partner, device_id_type=MESH
        )

    def quarters(region):
        return [around[region.axes[0]][step] for step in (2, 1, -1, 0)]

    def term_weight(region, matrix, position, remote):
        quarter = quarters(region)[position] if region.wave == 0 else None
        index = region.first + position
        sems = (w_own.at[index], shared.at[0], w_recv.at[index])
        return weight_copy(region, matrix, quarter, sems, remote)

    def wait_weights(region, position):
        start, size = weight_columns(region, quarters(region)[position] if region.wave == 0 else None)
        both = weights.at[pl.ds(0, 2), pl.ds(0, TILE), pl.ds(multiple(start, TILE), size)]
        drain(both, w_own.at[region.first + position])
        drain(both, w_recv.at[region.first + position])

    def down_weight(region, remote):
        return weight_copy(region, 2, None, (shared.at[1], shared.at[2], shared.at[3]), remote)

    def weight_order():
        for position in range(4):
            for region in regions:
                if region.wave == 0:
                    yield region, position
        for region in regions:
            if region.wave > 0:
                yield region, 0

    def token_copy(step):
        to = peers[step]
        return pltpu.make_async_remote_copy(
            src_ref=staged.at[lax.div(to, 2)],
            dst_ref=gathered.at[col],
            send_sem=exchange.at[0],
            recv_sem=exchange.at[1],
            device_id=(row, to),
            device_id_type=MESH,
        )

    def out_copy(step):
        to = peers[step]
        return pltpu.make_async_remote_copy(
            src_ref=parts.at[to],
            dst_ref=inbox.at[col],
            send_sem=exchange.at[2],
            recv_sem=exchange.at[3],
            device_id=(row, to),
            device_id_type=MESH,
        )

    others = pl.ds(0, cols - 1)

    def at_stage(region, stage, step=0):
        return around[region.axes[stage]][step]

    def rows_from(region, stage, step):
        if stage == 1:
            return multiple(at_stage(region, 1, step) * 64, 64)
        return multiple(at_stage(region, 1) * 64 + at_stage(region, 2, step) * 16, 16)

    def sums_view(region, stage, matrix, step):
        if stage == 0:
            return region.sums.at[matrix, at_stage(region, 0, step)]
        return region.sums.at[matrix, at_stage(region, 0), pl.ds(rows_from(region, stage, step), ROWS[stage])]

    def send_sums(region, stage, *slots):
        for slot in slots:
            step = STEP_OF[slot]
            pltpu.make_async_remote_copy(
                src_ref=sums_view(region, stage, GATE_OF[slot], step if slot < 4 else 2),
                dst_ref=region.boxes[stage].at[slot],
                send_sem=shared.at[4 + stage],
                recv_sem=red_recv.at[region.index * 7 + stage * 3 + max(slot - 3, 0)],
                device_id=near[region.axes[stage], step],
                device_id_type=MESH,
            ).start()

    def send_last(region):
        first = at_stage(region, 0)
        for slot, step in enumerate((2, 1, -1)):
            rows = pl.ds(rows_from(region, 2, step), ROWS[2])
            pltpu.make_async_remote_copy(
                src_ref=region.sums.at[:, first, rows],
                dst_ref=region.box3.at[slot],
                send_sem=shared.at[6],
                recv_sem=red_recv.at[region.index * 7 + 6],
                device_id=near[region.axes[2], step],
                device_id_type=MESH,
            ).start()

    def arrived(region, stage, group):
        box = region.boxes[stage]
        drain(box.at[pl.ds(0, 4)] if group == 0 else box.at[group + 3], red_recv.at[region.index * 7 + stage * 3 + group])

    def add_rows(target, *terms):
        count = target.shape[0] // 16
        together = min(count, 4)

        @pl.loop(0, count // together)
        def _(outer):
            for inner in range(together):
                at = pl.ds(multiple((outer * together + inner) * 16, 16), 16)
                value = target[at, :]
                for term in terms:
                    value = value + term[at, :]
                target[at, :] = value

    def terms(region, quarter):
        columns = pl.ds(multiple(region.offset + quarter * region.width, TILE), region.width)

        block = gathered[...].reshape(256, 256)
        for matrix in range(2):
            region.sums[matrix, quarter] = jnp.dot(
                block, weights[matrix, :, columns], preferred_element_type=jnp.float32
            ).astype(jnp.bfloat16)

    def task_first(region):
        wait_weights(region, 0)
        terms(region, quarters(region)[0])
        send_sums(region, 0, 4, 5)

    def task_second(region):
        for position, slot in ((1, 0), (2, 2), (3, None)):
            if region.wave == 0:
                wait_weights(region, position)
            terms(region, quarters(region)[position])
            if slot is not None:
                send_sums(region, 0, slot)

    def task_relay(stage):
        def run(region):
            for group, step, slot in ((1, 1, 1), (2, -1, 3)):
                arrived(region, stage, group)
                add_rows(sums_view(region, stage, group - 1, step), region.boxes[stage].at[group + 3])
                send_sums(region, stage, slot)

        return run

    def task_settle(stage):
        def run(region):
            arrived(region, stage, 0)
            box = region.boxes[stage]
            add_rows(sums_view(region, stage, 0, 0), box.at[1], box.at[2])
            add_rows(sums_view(region, stage, 1, 0), box.at[0], box.at[3])
            if stage == 0:
                send_sums(region, 1, 4, 5, 0, 2)
            else:
                send_last(region)

        return run

    def hidden_view(region, stage, step, part=None):
        size = ROWS[stage]
        if stage == 0:
            at, start = at_stage(region, 0, step), 0
            if part is None:
                return region.hidden.at[at]
        else:
            at, start = at_stage(region, 0), rows_from(region, stage, step)
        if part is not None:
            size //= 2
            start = start + part * size
        return region.hidden.at[at, pl.ds(start if isinstance(start, int) else multiple(start, 16), size)]

    def send_hidden(region, stage, *slots):
        for slot in slots:
            step = 1 if slot % 2 == 0 else -1
            view = hidden_view(region, stage, 0 if slot < 2 else -step, slot - 2 if slot >= 2 else None)
            pltpu.make_async_remote_copy(
                src_ref=view,
                dst_ref=view,
                send_sem=shared.at[7 + stage],
                recv_sem=all_recv.at[(region.index * 3 + stage) * 2 + slot // 2],
                device_id=near[region.axes[stage], step],
                device_id_type=MESH,
            ).start()

    def send_first(region):
        view = hidden_view(region, 2, 0)
        for step in (2, 1, -1):
            pltpu.make_async_remote_copy(
                src_ref=view,
                dst_ref=view,
                send_sem=shared.at[9],
                recv_sem=all_recv.at[(region.index * 3 + 2) * 2],
                device_id=near[region.axes[2], step],
                device_id_type=MESH,
            ).start()

    def hidden_rows(region, stage, count):
        if stage == 0 and count > 1:
            return region.hidden.at[pl.ds(0, count)]
        return region.hidden.at[0, pl.ds(0, ROWS[stage] * count)]

    def reached(region, stage, group):
        drain(hidden_rows(region, stage, 2 - group), all_recv.at[(region.index * 3 + stage) * 2 + group])

    def task_hidden(region):
        box = region.box3
        drain(box, red_recv.at[region.index * 7 + 6])
        at, rows = at_stage(region, 0), pl.ds(rows_from(region, 2, 0), ROWS[2])
        gate, up = (
            region.sums[matrix, at, rows].astype(jnp.float32)
            + box[0, matrix].astype(jnp.float32)
            + box[1, matrix].astype(jnp.float32)
            + box[2, matrix].astype(jnp.float32)
            for matrix in range(2)
        )
        hidden_view(region, 2, 0)[...] = (gate / (1.0 + jnp.exp(-gate)) * up).astype(jnp.bfloat16)
        send_first(region)

    def task_forward(stage):
        def run(region):
            reached(region, stage, 0)
            send_hidden(region, stage, 2, 3)
            if stage == 0:
                for step in (0, 1, -1):
                    project(region, at_stage(region, 0, step))

        return run

    def task_gathered(stage):
        def run(region):
            if stage == 2:
                drain(hidden_rows(region, 2, 3), all_recv.at[(region.index * 3 + 2) * 2])
            else:
                reached(region, stage, 1)
            send_hidden(region, stage - 1, 0, 1)

        return run

    def project(region, quarter):
        columns = pl.ds(multiple(region.offset + quarter * region.width, TILE), region.width)
        total[...] += lax.dot_general(
            region.hidden[quarter], weights[2, :, columns], (((1,), (1,)), ((), ())), preferred_element_type=jnp.float32
        )

    def task_project(region):
        reached(region, 0, 1)
        project(region, at_stage(region, 0, 2))

    first_product = task_forward(0)
    tasks = (
        task_first, task_second, task_relay(0), task_settle(0), task_relay(1), task_settle(1),
        task_hidden, task_gathered(2), task_forward(1), task_gathered(1), first_product, task_project,
    )

    for block in range(cols // 2):
        pltpu.make_async_copy(tokens.at[:, pl.ds(block * 256, 256)], staged.at[block], exchange.at[4]).start()
    for region, position in weight_order():
        for matrix in range(2):
            term_weight(region, matrix, position, False).start()
    drain(staged, exchange.at[4])

    barrier = pltpu.get_barrier_semaphore()
    for step in range(1, cols):
        pl.semaphore_signal(barrier, inc=1, device_id=(row, peers[step]), device_id_type=MESH)
    for axis in (1, 2):
        for step in (1, 2, -1):
            pl.semaphore_signal(barrier, inc=1, device_id=near[axis, step], device_id_type=MESH)
    pl.semaphore_wait(barrier, cols - 1 + 6)

    for step in range(1, cols):
        token_copy(step).start()
    for region, position in weight_order():
        for matrix in range(2):
            term_weight(region, matrix, position, True).start()
    for region in regions:
        down_weight(region, False).start()
        down_weight(region, True).start()

    total[...] = jnp.zeros_like(total)
    gathered[col] = staged[chip]
    drain(gathered.at[others], exchange.at[1])

    down_waited = False
    for wave, number in order_of(len(tasks)):
        if tasks[number] is first_product and not down_waited:
            down_waited = True
            for sem in (1, 3):
                drain(weights.at[2, pl.ds(0, TILE)], shared.at[sem])
        for region in regions:
            if region.wave == wave:
                tasks[number](region)

    parts[...] = total[...].astype(jnp.bfloat16).reshape(cols, 16, 256)
    for step in range(1, cols):
        out_copy(step).start()
    inbox[col] = parts[col]
    drain(inbox.at[others], exchange.at[3])
    for block in range(cols // 2):
        out[:, block * 256 : (block + 1) * 256] = (
            inbox[2 * block].astype(jnp.float32) + inbox[2 * block + 1].astype(jnp.float32)
        ).astype(jnp.bfloat16)

    drain(gathered.at[others], exchange.at[0])
    drain(parts.at[others], exchange.at[2])
    drain(weights.at[pl.ds(0, 2), pl.ds(0, TILE)], shared.at[0])
    drain(weights.at[2, pl.ds(0, TILE)], shared.at[2])
    drain(weights.at[:, pl.ds(0, 128)], shared.at[4])
    drain(weights.at[:, pl.ds(0, 32)], shared.at[5])
    drain(weights.at[:, pl.ds(0, 16), pl.ds(0, half // 2)], shared.at[6])
    drain(weights.at[0, pl.ds(0, 192)], shared.at[7])
    drain(weights.at[0, pl.ds(0, 48)], shared.at[8])
    drain(weights.at[0, pl.ds(0, 48), pl.ds(0, half // 4)], shared.at[9])


def on_device(tokens, gate_weight, up_weight, down_weight):
    batches, block, width = tokens.shape
    units = gate_weight.shape[1]
    half = units // 2
    regions = regions_of(half)
    count = len(regions)
    pieces = sum(region.pieces for region in regions)
    bf16 = jnp.bfloat16
    dma = pltpu.SemaphoreType.DMA

    scratch = [
        pltpu.VMEM((3, 256, half), bf16),
        pltpu.VMEM((16, 16, 256), bf16),
        pltpu.VMEM((16, 16, 256), bf16),
        pltpu.VMEM((16, 16, 256), bf16),
        pltpu.VMEM((256, 256), jnp.float32),
        dma((5,)), dma((10,)), dma((pieces,)), dma((pieces,)), dma((count * 7,)), dma((count * 6,)),
    ]
    for region in regions:
        w = region.width
        scratch += [
            pltpu.VMEM((2, 4, 256, w), bf16),
            pltpu.VMEM((6, 256, w), bf16),
            pltpu.VMEM((6, 64, w), bf16),
            pltpu.VMEM((3, 2, 16, w), bf16),
            pltpu.VMEM((4, 256, w), bf16),
        ]

    scratch.append(pltpu.VMEM((8, 16, 256), bf16))
    anywhere = pl.BlockSpec(memory_space=pl.ANY)
    out = pl.pallas_call(
        lambda *refs: kernel(regions, half, *refs),
        out_shape=jax.ShapeDtypeStruct((batches * block, width), bf16),
        in_specs=[anywhere] * 4,
        out_specs=pl.BlockSpec(memory_space=pltpu.VMEM),
        scratch_shapes=scratch,
        name="ffn",
        compiler_params=pltpu.CompilerParams(
            collective_id=0, has_side_effects=True, vmem_limit_bytes=67_000_000
        ),
    )(tokens.reshape(batches * block, width), gate_weight, up_weight, down_weight)
    return out.reshape(batches, block, width)


def solution(mesh):
    spread = P(("row", "col"), None)
    return jax.shard_map(
        on_device,
        mesh=mesh,
        in_specs=(P(None, "col", "row"), spread, spread, spread),
        out_specs=P(None, "col", "row"),
        check_vma=False,
    )
```
